32 devices in a mesh: pb: 4 (over y, x), db: 8 (over z, core).
Axes of the slice: x: 2, y: 2, z: 4, core: 2. Of those that a mesh axis runs over, the one named last changes fastest.
Arguments:
- slab: float32 [65536, 1024], P('db', 'pb'), may hold values from -6 to 6
- queries: float32 [128, 1024], P('db', 'pb'), may hold values from -6 to 6
- block_ids: int32 [128, 16], P('db'), may hold values from 0 to 4095, as said below
Outputs:
- scores: float32 [128, 256], P('db')
- gram: float32 [128, 256, 256], P('db', 'pb')
- penalty: float32 [128, 256, 256], P('db', 'pb')
The draws below stay inside these ranges and needn't reach their ends.
Inputs may be any that keep to these rules, and one draw needn't show every extreme that they name: `block_ids`: block id k lies in the slab rows of db index k // 512. Among the ids of the 16 queries of one db index, no db index is named more than 48 times, and one db index, the same for all db indices, is named exactly 48 times.
All inputs are finite; a program needn't handle non-finite values.
Results may differ from the reference program's by a relative error of at most 0.000096.
Values sent between devices are 32-bit elements; how exact they have to be, the bound alone decides.
No kernel may reach another device: no remote copies, remote signals or barrier semaphores. Data moves between devices by JAX's collectives and lax.ppermute only.
A program may use at most 128 MiB of HBM per device.

```python
import math
import jax
import jax.numpy as jnp
import numpy as np
from jax import lax

W = 1024
BLOCK = 16
NQB = 16
SLAB_DEV = 8192
Q_COL = 16
CAND = 256
ROWS = 65536
QUERIES = 128
N_DB = 8


def draw_block_ids(key, part):
    request_count = Q_COL * NQB
    capacity = 3 * request_count // (2 * N_DB)
    rest_ranks = np.repeat(np.arange(1, N_DB), capacity).astype(np.int32)
    key_popular, key_devices = jax.random.split(jax.random.fold_in(key, 7))
    popular = jax.random.permutation(key_popular, N_DB).astype(jnp.int32)
    blocks_each = SLAB_DEV // BLOCK

    def per_device(device_key):
        key_one, key_two, key_three = jax.random.split(device_key, 3)
        shuffled = jax.random.permutation(key_one, jnp.asarray(rest_ranks, jnp.int32))
        ranks = jnp.concatenate([jnp.zeros((capacity,), jnp.int32), shuffled[:request_count - capacity]])
        ranks = jax.random.permutation(key_two, ranks)
        owners = popular[ranks]
        local_block = jax.random.randint(key_three, (request_count,), 0, blocks_each).astype(jnp.int32)
        return (owners * blocks_each + local_block).reshape(Q_COL, NQB)
    device_keys = jax.random.split(key_devices, N_DB)
    return jax.vmap(per_device)(device_keys).reshape(Q_COL * N_DB, NQB).astype(jnp.int32)


def levels(stream_key, shape, cuts, least, top_value):
    def one(axis_at, blocks):
        steps = jax.random.uniform(jax.random.fold_in(jax.random.fold_in(stream_key, 6), axis_at), (blocks,), jnp.float32, least / len(cuts), top_value / len(cuts))
        return jnp.repeat(jnp.exp(steps), shape[axis_at] // blocks).reshape((-1,) + (1,) * (len(shape) - axis_at - 1))

    factor_of = one(*cuts[0])
    for cut in cuts[1:]:
        factor_of = factor_of * one(*cut)
    return factor_of


def normal_values(own_key, shape, deviation, limit, shards=(), kind=jnp.bfloat16):
    result = deviation * jax.random.normal(own_key, shape, jnp.float32)
    if shards:
        result = result * levels(own_key, shape, shards, -0.22, 0.18)
    return jnp.clip(result, -limit, limit).astype(kind)


def setup_inputs(seed: int = 0) -> dict:
    key_list = jax.random.split(jax.random.key(seed), 4)
    slab = normal_values(key_list[0], (ROWS, W), 1.0, 6.0, ((0, 8), (1, 4)), jnp.float32)
    queries = normal_values(key_list[1], (QUERIES, W), 1.0, 6.0, ((0, 8), (1, 4)), jnp.float32)
    block_ids = draw_block_ids(jax.random.fold_in(key_list[3], 71), 0)
    return dict(slab=slab, queries=queries, block_ids=block_ids)


epsilon = 1e-06

def reference(slab, queries, block_ids):
    slab_blocks = slab.reshape(-1, BLOCK, W)
    highest = lax.Precision.HIGHEST

    def per_query(pair):
        query_vec, query_ids = pair
        cand_rows = slab_blocks[query_ids].reshape(CAND, W)
        query_norm = jnp.sqrt(jnp.sum(query_vec * query_vec) + epsilon)
        row_norm = jnp.sqrt(lax.optimization_barrier(jnp.sum(cand_rows * cand_rows, axis=1)) + epsilon)
        query_dots = jnp.dot(cand_rows, query_vec, precision=highest)
        score_row = math.sqrt(W) * query_dots / (query_norm * row_norm)
        raw_gram = jnp.dot(cand_rows, cand_rows.T, precision=highest)
        gram_mat = raw_gram / (row_norm[:, None] * row_norm[None, :])
        penalty_mat = gram_mat * jax.nn.sigmoid(score_row[None, :] - score_row[:, None])
        return (score_row, gram_mat, penalty_mat)
    scores, gram, penalty = lax.map(per_query, (queries, block_ids))
    return (scores, gram, penalty)
```

```python
import functools
import math

import jax
import jax.numpy as jnp
from jax import lax
from jax.experimental import pallas as pl
from jax.experimental.pallas import tpu as pltpu
from jax.sharding import PartitionSpec as P

BLOCK = 16
STAT_ROWS = 8

epsilon = 1e-06


SMEM = pl.BlockSpec(memory_space=pltpu.SMEM)
VMEM = pl.BlockSpec(memory_space=pltpu.VMEM)
ANY = pl.BlockSpec(memory_space=pl.ANY)


def exchange(value, axis, offset):
    count = lax.axis_size(axis)
    return lax.ppermute(value, axis, [(i, i ^ offset) for i in range(count)])


def start_rows(table, slab, outs, sems, first, size):
    for k, out in enumerate(outs, 1):

        def body(s, carry, k=k, out=out):
            block = table[first + s, k]
            pltpu.make_async_copy(slab.at[block], out.at[s], sems.at[k]).start()
            return carry

        lax.fori_loop(0, size, body, 0, unroll=4)


def wait_rows(slab, outs, sems, size):
    for k, out in enumerate(outs, 1):
        pltpu.make_async_copy(slab.at[pl.ds(0, size)], out, sems.at[k]).wait()


def index_kernel(pos, ids, limit, slab, table, place, cum, late, *rest, dims, size):
    db_count, capacity, blocks_each, blocks_named, query_count = dims
    outs, (table_smem, table_sem, sems) = rest[:-3], rest[-3:]
    request_count = ids.shape[1]
    me = pos[0]
    all_ids = ids[...]
    owner = all_ids // blocks_each
    local = (all_ids - owner * blocks_each).astype(jnp.float32)
    owner_col = jnp.transpose(owner.astype(jnp.float32)).astype(jnp.int32)
    owner = owner.astype(jnp.int32)
    square = (request_count, request_count)
    before = lax.broadcasted_iota(jnp.int32, square, 0) < lax.broadcasted_iota(jnp.int32, square, 1)
    slot_col = lax.broadcasted_iota(jnp.int32, (capacity, 1), 0)
    tardy = jnp.zeros((1, request_count), jnp.int32)
    ranks = []
    for k in range(db_count):
        same = (owner_col[:, k : k + 1] == owner[k : k + 1, :]) & before
        rank = jnp.sum(jnp.where(same, 1.0, 0.0), axis=0, keepdims=True).astype(jnp.int32)
        ranks.append(rank)
        tardy = jnp.maximum(tardy, jnp.where(rank >= limit[...], 1, 0))
        mine = (rank == slot_col) & (owner[k : k + 1, :] == me)
        column = jnp.sum(jnp.where(mine, local[k : k + 1, :], 0.0), axis=1, keepdims=True)
        table[:, k : k + 1] = column.astype(jnp.int32)
    to_smem = pltpu.make_async_copy(table, table_smem, table_sem)
    to_smem.start()
    late[...] = jnp.max(tardy, axis=1, keepdims=True)
    request = lax.broadcasted_iota(jnp.int32, (1, request_count), 1)
    request_f = request.astype(jnp.float32)
    query_col = lax.broadcasted_iota(jnp.int32, (cum.shape[0], 1), 0)
    to_smem.wait()
    start_rows(table_smem, slab, outs, sems, 0, size)
    for k in range(db_count):
        asked = owner[0:1, :] == (me ^ k)
        mine = (ranks[0] == slot_col) & asked
        column = jnp.sum(jnp.where(mine, request_f, 0.0), axis=1, keepdims=True)
        place[:, k : k + 1] = column.astype(jnp.int32)
        early = (request < query_col * blocks_named) & asked
        column = jnp.sum(jnp.where(early, 1.0, 0.0), axis=1, keepdims=True)
        cum[:, k : k + 1] = column.astype(jnp.int32)
    wait_rows(slab, outs, sems, size)


def gather_kernel(table, slab, *rest, first, size):
    outs, sems = rest[:-1], rest[-1]
    start_rows(table, slab, outs, sems, first, size)
    wait_rows(slab, outs, sems, size)


def split(value):
    high = value.astype(jnp.bfloat16)
    low = (value - high.astype(jnp.float32)).astype(jnp.bfloat16)
    return high, low


def dot_rows(left, right):
    return lax.dot_general(
        left, right, (((1,), (1,)), ((), ())), preferred_element_type=jnp.float32
    )


def gram_kernel(
    pos, table, place, cum, late, queries, slab, *rest, dims, bounds, first_query, last_query, always
):
    db_count, capacity, blocks_each, blocks_named, query_count = dims
    partners = db_count - 1
    chunk_count = len(bounds) - 1
    received = rest[: partners * chunk_count]
    rest = rest[partners * chunk_count :]
    out_count = len(rest) - 3
    outs, (cand, whole, sem) = rest[:out_count], rest[out_count:]
    blocks = (last_query - first_query) * blocks_named
    base = first_query * blocks_named

    def fetch():
        for k in range(db_count):
            low = cum[first_query, k]
            high = cum[last_query, k]
            if k == 0:

                def body(s, carry):
                    source = slab.at[table[s, 0]]
                    pltpu.make_async_copy(source, cand.at[place[s, 0] - base], sem).start()
                    return carry

                lax.fori_loop(low, high, body, 0)
                continue
            for c in range(chunk_count):
                ref = received[c * partners + k - 1]

                def body(s, carry, ref=ref, k=k, c=c):
                    source = ref.at[s - bounds[c]]
                    pltpu.make_async_copy(source, cand.at[place[s, k] - base], sem).start()
                    return carry

                lax.fori_loop(
                    jnp.maximum(low, bounds[c]), jnp.minimum(high, bounds[c + 1]), body, 0
                )
        pltpu.make_async_copy(slab.at[pl.ds(0, blocks)], cand, sem).wait()

    if always:
        fetch()
    else:
        pl.when(late[0, 0] == 0)(fetch)

    rows = blocks_named * BLOCK
    own = rows // out_count
    width = slab.shape[2]
    me = pos[1]
    eye = lax.broadcasted_iota(jnp.int32, (rows, rows), 0) == lax.broadcasted_iota(
        jnp.int32, (rows, rows), 1
    )

    def one(q, carry):
        values = cand[pl.ds(q * blocks_named, blocks_named)].reshape(rows, width)
        query = queries[pl.ds(first_query + q, 1), :]
        query8 = jnp.broadcast_to(query, (STAT_ROWS, width))
        high, low = split(values)
        query_high, query_low = split(query8)
        gram = dot_rows(high, high) + (dot_rows(high, low) + dot_rows(low, high))
        dots = dot_rows(query_high, high) + (dot_rows(query_high, low) + dot_rows(query_low, high))
        whole[...] = gram
        squares = jnp.sum(jnp.where(eye, gram, 0.0), axis=0, keepdims=True)
        query_square = jnp.sum(query * query, axis=1, keepdims=True)
        row = lax.broadcasted_iota(jnp.int32, (STAT_ROWS, rows), 0)
        stats = jnp.where(row == 0, squares, jnp.where(row == 1, dots, query_square))
        for j, out in enumerate(outs):
            start = pl.multiple_of((me ^ j) * own, own)
            out[q, 0:own, :] = whole[pl.ds(start, own), :]
            out[q, own : own + STAT_ROWS, :] = stats
        return carry

    lax.fori_loop(0, last_query - first_query, one, 0)


def final_kernel(pos, *rest, first_query, full_width, parts, chained):
    inputs, rest = rest[:parts], rest[parts:]
    if chained:
        old_scores, rest = rest[0], rest[3:]
    scores, gram_out, penalty_out, columns = rest
    q = pl.program_id(0)
    own = gram_out.shape[1]
    level = [ref[0] for ref in inputs]
    while len(level) > 1:
        level = [level[i] + level[i + 1] for i in range(0, len(level), 2)]
    total = level[0]
    row_norm = jnp.sqrt(total[own : own + 1] + epsilon)
    query_norm = jnp.sqrt(total[own + 2 : own + 3] + epsilon)
    score = math.sqrt(full_width) * total[own + 1 : own + 2] / (query_norm * row_norm)
    row = lax.broadcasted_iota(jnp.int32, (STAT_ROWS, row_norm.shape[1]), 0)
    columns[...] = jnp.transpose(jnp.where(row == 0, row_norm, score))
    start = pl.multiple_of(pos[1] * own, own)
    mine = columns[pl.ds(start, own), :]
    gram = total[0:own] / (mine[:, 0:1] * row_norm)
    gram_out[0] = gram
    penalty_out[0] = gram / (1.0 + jnp.exp(mine[:, 1:2] - score))
    if chained:
        @pl.when(q == 0)
        def _():
            scores[...] = old_scores[...]
    scores[pl.ds(first_query + q, 1), :] = score


def per_device(slab, queries, block_ids):
    query_count, width_part = queries.shape
    db_count = lax.axis_size("db")
    pb_count = lax.axis_size("pb")
    blocks_named = block_ids.shape[1]
    cand_count = blocks_named * BLOCK
    own_count = cand_count // pb_count
    blocks_each = slab.shape[0] // BLOCK
    request_count = query_count * blocks_named
    capacity = 3 * request_count // (2 * db_count)
    partners = db_count - 1
    dims = (db_count, capacity, blocks_each, blocks_named, query_count)
    f32, i32 = jnp.float32, jnp.int32
    pos = jnp.stack([lax.axis_index("db"), lax.axis_index("pb")]).astype(i32)
    slab_blocks = slab.reshape(blocks_each, BLOCK, width_part)

    bounds = [0, capacity // 3, 2 * capacity // 3, 5 * capacity // 6, capacity]
    chunk_count = len(bounds) - 1
    groups = [
        (2, 0, 3 * query_count // 8),
        (3, 3 * query_count // 8, 5 * query_count // 8),
        (4, 5 * query_count // 8, query_count),
    ]
    limit = []
    for needed, first, last in groups:
        limit += [bounds[needed]] * ((last - first) * blocks_named)
    limit = jnp.asarray(limit, i32).reshape(1, request_count)

    ids = block_ids.reshape(1, request_count)
    step = 1
    while step < db_count:
        ids = jnp.concatenate([ids, exchange(ids, "db", step)], axis=0)
        step *= 2

    def chunk_shapes(size):
        return [jax.ShapeDtypeStruct((size, BLOCK, width_part), f32)] * partners

    size = bounds[1]
    outs = pl.pallas_call(
        functools.partial(index_kernel, dims=dims, size=size),
        in_specs=[SMEM, VMEM, VMEM, ANY],
        out_specs=[VMEM] * (4 + partners),
        out_shape=[
            jax.ShapeDtypeStruct((capacity, db_count), i32),
            jax.ShapeDtypeStruct((capacity, db_count), i32),
            jax.ShapeDtypeStruct((query_count + 8, db_count), i32),
            jax.ShapeDtypeStruct((1, 1), i32),
        ]
        + chunk_shapes(size),
        scratch_shapes=[
            pltpu.SMEM((capacity, db_count), i32),
            pltpu.SemaphoreType.DMA,
            pltpu.SemaphoreType.DMA((db_count,)),
        ],
        name="index",
    )(pos, ids, limit, slab_blocks)
    table, place, cum, late = outs[:4]
    chunks = [outs[4:]]
    for c in range(1, chunk_count):
        size = bounds[c + 1] - bounds[c]
        chunks.append(
            pl.pallas_call(
                functools.partial(gather_kernel, first=bounds[c], size=size),
                in_specs=[SMEM, ANY],
                out_specs=[VMEM] * partners,
                out_shape=chunk_shapes(size),
                scratch_shapes=[pltpu.SemaphoreType.DMA((db_count,))],
                name="gather",
            )(table, slab_blocks)
        )
    order = sorted(range(1, db_count), reverse=True)
    received = []
    for chunk in chunks:
        got = {k: exchange(chunk[k - 1], "db", k) for k in order}
        received.append([got[k] for k in range(1, db_count)])

    def gram_part(table, place, cum, late, received, needed, first, last, always):
        shape = (last - first, own_count + STAT_ROWS, cand_count)
        refs = [ref for got in received[:needed] for ref in got]
        return pl.pallas_call(
            functools.partial(
                gram_kernel,
                dims=dims,
                bounds=bounds[: needed + 1],
                first_query=first,
                last_query=last,
                always=always,
            ),
            in_specs=[SMEM] * 5 + [VMEM] + [ANY] * (1 + len(refs)),
            out_specs=[VMEM] * pb_count,
            out_shape=[jax.ShapeDtypeStruct(shape, f32)] * pb_count,
            scratch_shapes=[
                pltpu.VMEM(((last - first) * blocks_named, BLOCK, width_part), f32),
                pltpu.VMEM((cand_count, cand_count), f32),
                pltpu.SemaphoreType.DMA,
            ],
            name="gram",
        )(pos, table, place, cum, late, queries, slab_blocks, *refs)

    def finish(parts, first, last, old):
        parts = [parts[0]] + [exchange(parts[j], "pb", j) for j in range(1, pb_count)]
        part_spec = pl.BlockSpec((1, own_count + STAT_ROWS, cand_count), lambda q: (q, 0, 0))
        out_spec = pl.BlockSpec((1, own_count, cand_count), lambda q: (first + q, 0, 0))
        score_spec = pl.BlockSpec((query_count, cand_count), lambda q: (0, 0))
        out_shape = jax.ShapeDtypeStruct((query_count, own_count, cand_count), f32)
        extra = [] if old is None else [score_spec, ANY, ANY]
        aliases = {} if old is None else {pb_count + 2: 1, pb_count + 3: 2}
        return pl.pallas_call(
            functools.partial(
                final_kernel,
                first_query=first,
                full_width=width_part * pb_count,
                parts=pb_count,
                chained=old is not None,
            ),
            grid=(last - first,),
            in_specs=[SMEM] + [part_spec] * pb_count + extra,
            out_specs=[score_spec, out_spec, out_spec],
            out_shape=[jax.ShapeDtypeStruct((query_count, cand_count), f32), out_shape, out_shape],
            scratch_shapes=[pltpu.VMEM((cand_count, STAT_ROWS), f32)],
            input_output_aliases=aliases,
            name="final",
        )(pos, *parts, *(old or ()))

    results = None
    for needed, first, last in groups:
        parts = gram_part(table, place, cum, late, received, needed, first, last, False)
        results = finish(parts, first, last, results)

    def redo(results):
        parts = gram_part(
            table, place, cum, late, received, chunk_count, 0, query_count, True
        )
        return finish(parts, 0, query_count, None)

    return tuple(lax.cond(late[0, 0] > 0, redo, lambda kept: kept, results))


def solution(mesh):
    return jax.shard_map(
        per_device,
        mesh=mesh,
        in_specs=(P("db", "pb"), P("db", "pb"), P("db", None)),
        out_specs=(P("db", None), P("db", "pb", None), P("db", "pb", None)),
        check_vma=False,
    )
```

```python
import functools
import math

import jax
import jax.numpy as jnp
from jax import lax
from jax.experimental import pallas as pl
from jax.experimental.pallas import tpu as pltpu
from jax.sharding import PartitionSpec as P

BLOCK = 16
STAT_ROWS = 8

epsilon = 1e-06


SMEM = pl.BlockSpec(memory_space=pltpu.SMEM)
VMEM = pl.BlockSpec(memory_space=pltpu.VMEM)
ANY = pl.BlockSpec(memory_space=pl.ANY)


def exchange(value, axis, offset):
    count = lax.axis_size(axis)
    return lax.ppermute(value, axis, [(i, i ^ offset) for i in range(count)])


def start_rows(table, slab, outs, sems, first, size):
    for k, out in enumerate(outs, 1):

        def body(s, carry, k=k, out=out):
            block = table[first + s, k]
            pltpu.make_async_copy(slab.at[block], out.at[s], sems.at[k]).start()
            return carry

        lax.fori_loop(0, size, body, 0, unroll=4)


def wait_rows(slab, outs, sems, size):
    for k, out in enumerate(outs, 1):
        pltpu.make_async_copy(slab.at[pl.ds(0, size)], out, sems.at[k]).wait()


def index_kernel(pos, ids, limit, slab, table, place, cum, pool, late, *rest, dims, base, size):
    db_count, capacity, blocks_each, blocks_named, query_count = dims
    outs, (table_smem, table_sem, sems) = rest[:-3], rest[-3:]
    request_count = ids.shape[1]
    pool_size = pool.shape[0]
    me = pos[0]
    all_ids = ids[...]
    owner = all_ids // blocks_each
    local = (all_ids - owner * blocks_each).astype(jnp.float32)
    owner_col = jnp.transpose(owner.astype(jnp.float32)).astype(jnp.int32)
    code = (owner ^ me).astype(jnp.float32) * blocks_each + local
    square = (request_count, request_count)
    before = lax.broadcasted_iota(jnp.int32, square, 0) < lax.broadcasted_iota(jnp.int32, square, 1)
    slot_col = lax.broadcasted_iota(jnp.int32, (capacity, 1), 0)
    pool_col = lax.broadcasted_iota(jnp.int32, (pool_size, 1), 0)
    db_col = lax.broadcasted_iota(jnp.int32, (db_count, 1), 0)
    tardy = jnp.zeros((1, request_count), jnp.float32)

    def pick(mask, values, axis):
        return jnp.sum(jnp.where(mask, values, 0.0), axis=axis, keepdims=True)

    kept = []
    for k in range(db_count):
        own = owner[k : k + 1, :]
        same = (owner_col[:, k : k + 1] == own) & before
        rank = pick(same, 1.0, 0)
        beyond = jnp.maximum(pick(own == db_col, 1.0, 1) - base, 0.0)
        beyond = jnp.where(db_col == (me ^ k), 0.0, beyond)
        pooled = pick(db_col == own, beyond, 0)
        pool_slot = jnp.where(rank < pooled, rank + pick(db_col < own, beyond, 0), -1.0)
        pool_slot = pool_slot.astype(jnp.int32)
        slot = (rank - pooled).astype(jnp.int32)
        kept.append((slot, pool_slot))
        missed = (own != (me ^ k)) & (slot >= limit[...])
        total = jnp.sum(beyond, axis=0, keepdims=True)
        tardy = jnp.maximum(tardy, jnp.where(missed | (total > pool_size), 1.0, 0.0))
        mine = (slot == slot_col) & (own == me)
        table[:, k : k + 1] = pick(mine, local[k : k + 1, :], 1).astype(jnp.int32)
    to_smem = pltpu.make_async_copy(table, table_smem, table_sem)
    to_smem.start()
    late[...] = jnp.max(tardy, axis=1, keepdims=True).astype(jnp.int32)
    request = lax.broadcasted_iota(jnp.int32, (1, request_count), 1)
    request_f = request.astype(jnp.float32)
    query_col = lax.broadcasted_iota(jnp.int32, (cum.shape[0], 1), 0)
    to_smem.wait()
    start_rows(table_smem, slab, outs, sems, 0, size)
    slot, pool_slot = kept[0]
    own = owner[0:1, :]
    for k in range(db_count):
        asked = own == (me ^ k)
        mine = (slot == slot_col) & asked
        place[:, k : k + 1] = pick(mine, request_f, 1).astype(jnp.int32)
        early = (request < query_col * blocks_named) & asked & (slot >= 0)
        cum[:, k : k + 1] = pick(early, 1.0, 1).astype(jnp.int32)
        listed = kept[k][1] == pool_col
        pool[:, k : k + 1] = pick(listed, code[k : k + 1, :], 1).astype(jnp.int32)
    pool[:, db_count : db_count + 1] = pick(pool_slot == pool_col, request_f, 1).astype(jnp.int32)
    wait_rows(slab, outs, sems, size)


def pool_kernel(pool, slab, *rest, dims, step):
    blocks_each = dims[2]
    earlier, (out, sems) = rest[:step], rest[step:]
    pool_size = pool.shape[0]
    for m in range(out.shape[0]):
        k = (1 << step) + m * (2 << step)

        def body(v, carry, m=m, k=k):
            away = pool[v, k] // blocks_each
            target = out.at[m, v]
            found = jnp.int32(0)
            for s, ref in enumerate(earlier):
                here = (away >> s) == 1

                @pl.when(here)
                def _(ref=ref, s=s):
                    source = ref.at[k >> (s + 1), v]
                    pltpu.make_async_copy(source, target, sems.at[m]).start()

                found = found + here.astype(jnp.int32)

            @pl.when(found == 0)
            def _():
                block = pool[v, k] - away * blocks_each
                pltpu.make_async_copy(slab.at[block], target, sems.at[m]).start()

            return carry

        lax.fori_loop(0, pool_size, body, 0)
    for m in range(out.shape[0]):
        pltpu.make_async_copy(slab.at[pl.ds(0, pool_size)], out.at[m], sems.at[m]).wait()


def gather_kernel(table, slab, *rest, first, size):
    outs, sems = rest[:-1], rest[-1]
    start_rows(table, slab, outs, sems, first, size)
    wait_rows(slab, outs, sems, size)


def split(value):
    high = value.astype(jnp.bfloat16)
    low = (value - high.astype(jnp.float32)).astype(jnp.bfloat16)
    return high, low


def dot_rows(left, right):
    return lax.dot_general(
        left, right, (((1,), (1,)), ((), ())), preferred_element_type=jnp.float32
    )


def gram_kernel(
    pos, table, place, cum, pool, late, queries, slab, *rest, dims, bounds, first_query, last_query
):
    db_count, capacity, blocks_each, blocks_named, query_count = dims
    partners = db_count - 1
    chunk_count = len(bounds) - 1 if bounds else 0
    steps = db_count.bit_length() - 1 if bounds else 1
    received = rest[: partners * chunk_count]
    pooled = rest[partners * chunk_count : partners * chunk_count + steps]
    rest = rest[partners * chunk_count + steps :]
    out_count = len(rest) - 3
    outs, (cand, whole, sems) = rest[:out_count], rest[out_count:]
    group = last_query - first_query
    blocks = group * blocks_named
    first_request = first_query * blocks_named

    def fetch():
        def copy(source, request):
            to = request - first_request
            pltpu.make_async_copy(source, cand.at[to], sems.at[to // blocks_named]).start()

        for k in range(db_count):
            low = cum[first_query, k]
            high = cum[last_query, k]
            if k == 0:

                def body(s, carry):
                    copy(slab.at[table[s, 0]], place[s, 0])
                    return carry

                lax.fori_loop(low, high, body, 0)
                continue
            for c in range(chunk_count):

                def body(s, carry, ref=received[c * partners + k - 1], k=k, c=c):
                    copy(ref.at[s - bounds[c]], place[s, k])
                    return carry

                lax.fori_loop(
                    jnp.maximum(low, bounds[c]), jnp.minimum(high, bounds[c + 1]), body, 0
                )

        def listed(v, carry):
            away = pool[v, 0] // blocks_each
            request = pool[v, db_count]
            inside = (request >= first_request) & (request < first_request + blocks)
            for s, ref in enumerate(pooled):

                @pl.when(((away >> s) == 1) & inside)
                def _(ref=ref):
                    copy(ref.at[0, v], request)

            return carry

        lax.fori_loop(0, pool.shape[0], listed, 0)

    def arrived(q):
        part = cand.at[pl.ds(q * blocks_named, blocks_named)]
        pltpu.make_async_copy(slab.at[pl.ds(0, blocks_named)], part, sems.at[q]).wait()

    if bounds:
        complete = late[0, 0] == 0
        pl.when(complete)(fetch)
    else:
        for q in range(group):
            source = pooled[0].at[pl.ds(first_request + q * blocks_named, blocks_named)]
            part = cand.at[pl.ds(q * blocks_named, blocks_named)]
            pltpu.make_async_copy(source, part, sems.at[q]).start()

    rows = blocks_named * BLOCK
    own = rows // out_count
    width = slab.shape[2]
    me = pos[1]
    eye = lax.broadcasted_iota(jnp.int32, (rows, rows), 0) == lax.broadcasted_iota(
        jnp.int32, (rows, rows), 1
    )

    def one(q, carry):
        if bounds:
            pl.when(complete)(functools.partial(arrived, q))
        else:
            arrived(q)
        values = cand[pl.ds(q * blocks_named, blocks_named)].reshape(rows, width)
        query = queries[pl.ds(first_query + q, 1), :]
        query8 = jnp.broadcast_to(query, (STAT_ROWS, width))
        high, low = split(values)
        query_high, query_low = split(query8)
        gram = dot_rows(high, high) + (dot_rows(high, low) + dot_rows(low, high))
        dots = dot_rows(query_high, high) + (dot_rows(query_high, low) + dot_rows(query_low, high))
        whole[...] = gram
        squares = jnp.sum(jnp.where(eye, gram, 0.0), axis=0, keepdims=True)
        query_square = jnp.sum(query * query, axis=1, keepdims=True)
        row = lax.broadcasted_iota(jnp.int32, (STAT_ROWS, rows), 0)
        stats = jnp.where(row == 0, squares, jnp.where(row == 1, dots, query_square))
        for j, out in enumerate(outs):
            start = pl.multiple_of((me ^ j) * own, own)
            out[q, 0:own, :] = whole[pl.ds(start, own), :]
            out[q, own : own + STAT_ROWS, :] = stats
        return carry

    lax.fori_loop(0, group, one, 0)


def final_kernel(pos, *rest, first_query, full_width, parts, chained):
    inputs, rest = rest[:parts], rest[parts:]
    if chained:
        old_scores, rest = rest[0], rest[3:]
    scores, gram_out, penalty_out, columns = rest
    step = pl.program_id(0)
    count, own, _ = gram_out.shape
    if chained:

        @pl.when(step == 0)
        def _():
            scores[...] = old_scores[...]

    for q in range(count):
        level = [ref[q] for ref in inputs]
        while len(level) > 1:
            level = [level[i] + level[i + 1] for i in range(0, len(level), 2)]
        total = level[0]
        row_norm = jnp.sqrt(total[own : own + 1] + epsilon)
        query_norm = jnp.sqrt(total[own + 2 : own + 3] + epsilon)
        score = math.sqrt(full_width) * total[own + 1 : own + 2] / (query_norm * row_norm)
        row = lax.broadcasted_iota(jnp.int32, (STAT_ROWS, row_norm.shape[1]), 0)
        columns[q] = jnp.transpose(jnp.where(row == 0, row_norm, score))
        start = pl.multiple_of(pos[1] * own, own)
        mine = columns[q, pl.ds(start, own), :]
        gram = total[0:own] / (mine[:, 0:1] * row_norm)
        gram_out[q] = gram
        penalty_out[q] = gram / (1.0 + jnp.exp(mine[:, 1:2] - score))
        scores[pl.ds(first_query + step * count + q, 1), :] = score


def padded_rows(slab_blocks, block_ids, capacity):
    db_count = lax.axis_size("db")
    blocks_each = slab_blocks.shape[0]
    flat_ids = block_ids.reshape(-1)
    owners = flat_ids // blocks_each
    local_block = flat_ids % blocks_each
    onehot = (owners[:, None] == jnp.arange(db_count, dtype=jnp.int32)[None, :]).astype(jnp.int32)
    slot_index = jnp.sum((jnp.cumsum(onehot, axis=0) - 1) * onehot, axis=1)
    requests = jnp.zeros((db_count, capacity), jnp.int32).at[owners, slot_index].set(local_block)
    found = slab_blocks[lax.all_to_all(requests, "db", split_axis=0, concat_axis=0, tiled=True)]
    replies = lax.all_to_all(found, "db", split_axis=0, concat_axis=0, tiled=True)
    flat_replies = replies.reshape((db_count * capacity,) + slab_blocks.shape[1:])
    return flat_replies[owners * capacity + slot_index]


def per_device(slab, queries, block_ids):
    query_count, width_part = queries.shape
    db_count = lax.axis_size("db")
    pb_count = lax.axis_size("pb")
    blocks_named = block_ids.shape[1]
    cand_count = blocks_named * BLOCK
    own_count = cand_count // pb_count
    blocks_each = slab.shape[0] // BLOCK
    request_count = query_count * blocks_named
    capacity = 3 * request_count // (2 * db_count)
    base = 2 * capacity // 3
    pool_size = request_count // 9
    partners = db_count - 1
    steps = db_count.bit_length() - 1
    dims = (db_count, capacity, blocks_each, blocks_named, query_count)
    f32, i32 = jnp.float32, jnp.int32
    pos = jnp.stack([lax.axis_index("db"), lax.axis_index("pb")]).astype(i32)
    slab_blocks = slab.reshape(blocks_each, BLOCK, width_part)

    bounds = [0, base // 4, 5 * base // 8, 7 * base // 8, base]
    chunk_count = len(bounds) - 1
    groups = [
        (2, 0, 3 * query_count // 8),
        (3, 3 * query_count // 8, 5 * query_count // 8),
        (4, 5 * query_count // 8, query_count),
    ]
    limit = []
    for needed, first, last in groups:
        limit += [bounds[needed]] * ((last - first) * blocks_named)
    limit = jnp.asarray(limit, i32).reshape(1, request_count)

    ids = block_ids.reshape(1, request_count)
    for step in range(steps):
        ids = jnp.concatenate([ids, exchange(ids, "db", 1 << step)], axis=0)

    def blocks_shape(*sizes):
        return jax.ShapeDtypeStruct(sizes + (BLOCK, width_part), f32)

    size = bounds[1]
    outs = pl.pallas_call(
        functools.partial(index_kernel, dims=dims, base=base, size=size),
        in_specs=[SMEM, VMEM, VMEM, ANY],
        out_specs=[VMEM] * (5 + partners),
        out_shape=[
            jax.ShapeDtypeStruct((capacity, db_count), i32),
            jax.ShapeDtypeStruct((capacity, db_count), i32),
            jax.ShapeDtypeStruct((query_count + 8, db_count), i32),
            jax.ShapeDtypeStruct((pool_size, db_count + 1), i32),
            jax.ShapeDtypeStruct((1, 1), i32),
        ]
        + [blocks_shape(size)] * partners,
        scratch_shapes=[
            pltpu.SMEM((capacity, db_count), i32),
            pltpu.SemaphoreType.DMA,
            pltpu.SemaphoreType.DMA((db_count,)),
        ],
        name="index",
    )(pos, ids, limit, slab_blocks)
    table, place, cum, pool, late = outs[:5]
    order = sorted(range(1, db_count), reverse=True)

    def send(chunk):
        got = {k: exchange(chunk[k - 1], "db", k) for k in order}
        return [got[k] for k in range(1, db_count)]

    def gather(c, after):
        first, size = bounds[c], bounds[c + 1] - bounds[c]
        tied, _ = lax.optimization_barrier((table, after))
        return pl.pallas_call(
            functools.partial(gather_kernel, first=first, size=size),
            in_specs=[SMEM, ANY],
            out_specs=[VMEM] * partners,
            out_shape=[blocks_shape(size)] * partners,
            scratch_shapes=[pltpu.SemaphoreType.DMA((db_count,))],
            name="gather",
        )(tied, slab_blocks)

    def pool_step(step, pooled, after):
        lists = db_count >> (step + 1)
        tied, _ = lax.optimization_barrier((pool, after))
        out = pl.pallas_call(
            functools.partial(pool_kernel, dims=dims, step=step),
            in_specs=[SMEM] + [ANY] * (1 + step),
            out_specs=VMEM,
            out_shape=blocks_shape(lists, pool_size),
            scratch_shapes=[pltpu.SemaphoreType.DMA((lists,))],
            name="pool",
        )(tied, slab_blocks, *pooled)
        return out

    received = [send(outs[5:])]
    pooled = []
    out = pool_step(0, pooled, late)
    pooled.append(exchange(out, "db", 1))
    chunk = gather(1, out)
    received.append(send(chunk))
    for step in range(1, steps):
        out = pool_step(step, pooled, chunk[0])
        pooled.append(exchange(out, "db", 1 << step))
    chunk = gather(2, out)
    received.append(send(chunk))
    chunk = gather(3, (chunk[0], received[0]))
    received.append(send(chunk))

    def gram_part(bounds, refs, first, last):
        shape = (last - first, own_count + STAT_ROWS, cand_count)
        return pl.pallas_call(
            functools.partial(
                gram_kernel,
                dims=dims,
                bounds=bounds,
                first_query=first,
                last_query=last,
            ),
            in_specs=[SMEM] * 6 + [VMEM] + [ANY] * (1 + len(refs)),
            out_specs=[VMEM] * pb_count,
            out_shape=[jax.ShapeDtypeStruct(shape, f32)] * pb_count,
            scratch_shapes=[
                pltpu.VMEM(((last - first) * blocks_named, BLOCK, width_part), f32),
                pltpu.VMEM((cand_count, cand_count), f32),
                pltpu.SemaphoreType.DMA((last - first,)),
            ],
            name="gram",
        )(pos, table, place, cum, pool, late, queries, slab_blocks, *refs)

    def finish(parts, first, last, old):
        parts = [parts[0]] + [exchange(parts[j], "pb", j) for j in range(1, pb_count)]
        each = 2 - (last - first) % 2
        part_spec = pl.BlockSpec((each, own_count + STAT_ROWS, cand_count), lambda q: (q, 0, 0))
        out_spec = pl.BlockSpec(
            (each, own_count, cand_count), lambda q: (first // each + q, 0, 0)
        )
        score_spec = pl.BlockSpec((query_count, cand_count), lambda q: (0, 0))
        out_shape = jax.ShapeDtypeStruct((query_count, own_count, cand_count), f32)
        extra = [] if old is None else [score_spec, ANY, ANY]
        aliases = {} if old is None else {pb_count + 2: 1, pb_count + 3: 2}
        return pl.pallas_call(
            functools.partial(
                final_kernel,
                first_query=first,
                full_width=width_part * pb_count,
                parts=pb_count,
                chained=old is not None,
            ),
            grid=((last - first) // each,),
            in_specs=[SMEM] + [part_spec] * pb_count + extra,
            out_specs=[score_spec, out_spec, out_spec],
            out_shape=[jax.ShapeDtypeStruct((query_count, cand_count), f32), out_shape, out_shape],
            scratch_shapes=[pltpu.VMEM((each, cand_count, STAT_ROWS), f32)],
            input_output_aliases=aliases,
            name="final",
        )(pos, *parts, *(old or ()))

    results = None
    for needed, first, last in groups:
        refs = [ref for got in received[:needed] for ref in got] + pooled
        parts = gram_part(bounds[: needed + 1], refs, first, last)
        results = finish(parts, first, last, results)

    def redo(results):
        rows = padded_rows(slab_blocks, block_ids, capacity)
        parts = gram_part(None, [rows], 0, query_count)
        return finish(parts, 0, query_count, None)

    return tuple(lax.cond(late[0, 0] > 0, redo, lambda kept: kept, results))


def solution(mesh):
    return jax.shard_map(
        per_device,
        mesh=mesh,
        in_specs=(P("db", "pb"), P("db", "pb"), P("db", None)),
        out_specs=(P("db", None), P("db", "pb", None), P("db", "pb", None)),
        check_vma=False,
    )
```

```python
import functools
import math

import jax
import jax.numpy as jnp
from jax import lax
from jax.experimental import pallas as pl
from jax.experimental.pallas import tpu as pltpu
from jax.sharding import PartitionSpec as P


BLOCK = 16
STAT_ROWS = 8

epsilon = 1e-06


SMEM = pl.BlockSpec(memory_space=pltpu.SMEM)
VMEM = pl.BlockSpec(memory_space=pltpu.VMEM)
ANY = pl.BlockSpec(memory_space=pl.ANY)
PARAMS = pltpu.CompilerParams(vmem_limit_bytes=24 * 2**20)


def exchange(value, axis, offset):
    count = lax.axis_size(axis)
    return lax.ppermute(value, axis, [(i, i ^ offset) for i in range(count)])


def start_rows(table, slab, outs, sems, first, size):
    def body(s, carry):
        for k, out in enumerate(outs, 1):
            block = table[first + s, k]
            pltpu.make_async_copy(slab.at[block], out.at[s], sems.at[k]).start()
        return carry

    lax.fori_loop(0, size, body, 0)


def wait_rows(slab, outs, sems, size):
    for k, out in enumerate(outs, 1):
        pltpu.make_async_copy(slab.at[pl.ds(0, size)], out, sems.at[k]).wait()


def index_kernel(pos, ids, limit, slab, table, place, cum, pool, late, *rest, dims, base, size):
    db_count, capacity, blocks_each, blocks_named, _ = dims
    outs, (table_smem, table_sem, sems) = rest[:-3], rest[-3:]
    request_count = ids.shape[1]
    pool_size = pool.shape[0]
    me = pos[0]
    all_ids = ids[...]
    owner = all_ids // blocks_each
    local = (all_ids - owner * blocks_each).astype(jnp.float32)
    owner_col = jnp.transpose(owner.astype(jnp.float32)).astype(jnp.int32)
    code = (owner ^ me).astype(jnp.float32) * blocks_each + local
    square = (request_count, request_count)
    before = lax.broadcasted_iota(jnp.int32, square, 0) < lax.broadcasted_iota(jnp.int32, square, 1)
    slot_col = lax.broadcasted_iota(jnp.int32, (capacity, 1), 0)
    pool_col = lax.broadcasted_iota(jnp.int32, (pool_size, 1), 0)
    db_col = lax.broadcasted_iota(jnp.int32, (db_count, 1), 0)
    tardy = jnp.zeros((1, request_count), jnp.float32)

    def pick(mask, values, axis):
        return jnp.sum(jnp.where(mask, values, 0.0), axis=axis, keepdims=True)

    kept = []
    for k in range(db_count):
        own = owner[k : k + 1, :]
        same = (owner_col[:, k : k + 1] == own) & before
        rank = pick(same, 1.0, 0)
        beyond = jnp.maximum(pick(own == db_col, 1.0, 1) - base, 0.0)
        beyond = jnp.where(db_col == (me ^ k), 0.0, beyond)
        pooled = pick(db_col == own, beyond, 0)
        pool_slot = jnp.where(rank < pooled, rank + pick(db_col < own, beyond, 0), -1.0)
        pool_slot = pool_slot.astype(jnp.int32)
        slot = (rank - pooled).astype(jnp.int32)
        kept.append((slot, pool_slot))
        missed = (own != (me ^ k)) & (slot >= limit[...])
        total = jnp.sum(beyond, axis=0, keepdims=True)
        tardy = jnp.maximum(tardy, jnp.where(total > pool_size, 2.0, jnp.where(missed, 1.0, 0.0)))
        mine = (slot == slot_col) & (own == me)
        table[:, k : k + 1] = pick(mine, local[k : k + 1, :], 1).astype(jnp.int32)
    to_smem = pltpu.make_async_copy(table, table_smem, table_sem)
    to_smem.start()
    late[...] = jnp.max(tardy, axis=1, keepdims=True).astype(jnp.int32)
    request = lax.broadcasted_iota(jnp.int32, (1, request_count), 1)
    request_f = request.astype(jnp.float32)
    query_col = lax.broadcasted_iota(jnp.int32, (cum.shape[0], 1), 0)
    to_smem.wait()
    start_rows(table_smem, slab, outs, sems, 0, size)
    slot, pool_slot = kept[0]
    own = owner[0:1, :]
    for k in range(db_count):
        asked = own == (me ^ k)
        mine = (slot == slot_col) & asked
        place[:, k : k + 1] = pick(mine, request_f, 1).astype(jnp.int32)
        early = (request < query_col * blocks_named) & asked & (slot >= 0)
        cum[:, k : k + 1] = pick(early, 1.0, 1).astype(jnp.int32)
        listed = kept[k][1] == pool_col
        pool[:, k : k + 1] = pick(listed, code[k : k + 1, :], 1).astype(jnp.int32)
    pool[:, db_count : db_count + 1] = pick(pool_slot == pool_col, request_f, 1).astype(jnp.int32)
    wait_rows(slab, outs, sems, size)


def pool_kernel(pool, slab, *rest, dims, step):
    blocks_each = dims[2]
    earlier, (out, sems) = rest[:step], rest[step:]
    pool_size = pool.shape[0]

    def body(v, carry):
        for m in range(out.shape[0]):
            k = (1 << step) + m * (2 << step)
            code = pool[v, k]
            away = lax.div(code, blocks_each)
            target = out.at[m, v]
            found = jnp.int32(0)
            for s, ref in enumerate(earlier):
                here = (away >> s) == 1

                @pl.when(here)
                def _():
                    source = ref.at[k >> (s + 1), v]
                    pltpu.make_async_copy(source, target, sems.at[m]).start()

                found = found + here.astype(jnp.int32)

            def local():
                block = code - away * blocks_each
                pltpu.make_async_copy(slab.at[block], target, sems.at[m]).start()

            if earlier:
                pl.when(found == 0)(local)
            else:
                local()
        return carry

    lax.fori_loop(0, pool_size, body, 0)
    for m in range(out.shape[0]):
        pltpu.make_async_copy(slab.at[pl.ds(0, pool_size)], out.at[m], sems.at[m]).wait()


def gather_kernel(table, slab, *rest, first, size):
    outs, sems = rest[:-1], rest[-1]
    start_rows(table, slab, outs, sems, first, size)
    wait_rows(slab, outs, sems, size)


def own_kernel(table, slab, out, sem):
    def body(s, carry):
        pltpu.make_async_copy(slab.at[table[s, 0]], out.at[s], sem).start()
        return carry

    lax.fori_loop(0, out.shape[0], body, 0)
    pltpu.make_async_copy(slab.at[pl.ds(0, out.shape[0])], out, sem).wait()


def split(value):
    high = value.astype(jnp.bfloat16)
    low = (value - high.astype(jnp.float32)).astype(jnp.bfloat16)
    return high, low


def dot_rows(left, right):
    return lax.dot_general(
        left, right, (((1,), (1,)), ((), ())), preferred_element_type=jnp.float32
    )


def gram_kernel(pos, place, cum, pool, queries, own_rows, *rest, dims, bounds, first_query, last_query):
    db_count, capacity, blocks_each, blocks_named, _ = dims
    partners = db_count - 1
    chunk_count = len(bounds) - 1 if bounds else 0
    steps = db_count.bit_length() - 1 if bounds else 0
    received = rest[: partners * chunk_count]
    pooled = rest[partners * chunk_count : partners * chunk_count + steps]
    rest = rest[partners * chunk_count + steps :]
    out_count = len(rest) - 3
    outs, (high, low, whole) = rest[:out_count], rest[out_count:]
    group = last_query - first_query
    blocks = group * blocks_named
    first_request = first_query * blocks_named

    def keep(block, request):
        to = request - first_request
        block_high, block_low = split(block)
        high[to] = block_high
        low[to] = block_low

    if bounds:
        for k in range(db_count):
            begin = cum[first_query, k]
            end = cum[last_query, k]
            for c in range(chunk_count):
                if k == 0 and c > 0:
                    break
                ref = received[c * partners + k - 1] if k else own_rows
                base = bounds[c]
                top = bounds[c + 1] if k else capacity

                def body(s, carry, ref=ref, base=base, k=k):
                    keep(ref[s - base], place[s, k])
                    return carry

                lax.fori_loop(jnp.maximum(begin, base), jnp.minimum(end, top), body, 0)

        def listed(v, carry):
            away = lax.div(pool[v, 0], blocks_each)
            request = pool[v, db_count]
            inside = (request >= first_request) & (request < first_request + blocks)
            for s, ref in enumerate(pooled):

                @pl.when(((away >> s) == 1) & inside)
                def _():
                    keep(ref[0, v], request)

            return carry

        lax.fori_loop(0, pool.shape[0], listed, 0)
    else:

        def body(s, carry):
            keep(own_rows[first_request + s], first_request + s)
            return carry

        lax.fori_loop(0, blocks, body, 0)

    rows = blocks_named * BLOCK
    own = rows // out_count
    width = own_rows.shape[2]
    me = pos[1]
    square = (rows, rows)
    eye = lax.broadcasted_iota(jnp.int32, square, 0) == lax.broadcasted_iota(jnp.int32, square, 1)

    def one(q, carry):
        part = pl.ds(q * blocks_named, blocks_named)
        rows_high = high[part].reshape(rows, width)
        rows_low = low[part].reshape(rows, width)
        query = queries[pl.ds(first_query + q, 1), :]
        query_high, query_low = split(jnp.broadcast_to(query, (STAT_ROWS, width)))
        gram = dot_rows(rows_high, rows_high) + (
            dot_rows(rows_high, rows_low) + dot_rows(rows_low, rows_high)
        )
        dots = dot_rows(query_high, rows_high) + (
            dot_rows(query_high, rows_low) + dot_rows(query_low, rows_high)
        )
        whole[...] = gram
        squares = jnp.sum(jnp.where(eye, gram, 0.0), axis=0, keepdims=True)
        query_square = jnp.sum(query * query, axis=1, keepdims=True)
        row = lax.broadcasted_iota(jnp.int32, (STAT_ROWS, rows), 0)
        stats = jnp.where(row == 0, squares, jnp.where(row == 1, dots, query_square))
        for j, out in enumerate(outs):
            start = pl.multiple_of((me ^ j) * own, own)
            out[q, 0:own, :] = whole[pl.ds(start, own), :]
            out[q, own : own + STAT_ROWS, :] = stats
        return carry

    lax.fori_loop(0, group, one, 0)


def final_kernel(pos, *rest, first_query, full_width, parts, chained):
    inputs, rest = rest[:parts], rest[parts:]
    if chained:
        old_scores, rest = rest[0], rest[3:]
    scores, gram_out, penalty_out, columns = rest
    step = pl.program_id(0)
    count, own, _ = gram_out.shape
    if chained:

        @pl.when(step == 0)
        def _():
            scores[...] = old_scores[...]

    for q in range(count):
        level = [ref[q] for ref in inputs]
        while len(level) > 1:
            level = [level[i] + level[i + 1] for i in range(0, len(level), 2)]
        total = level[0]
        row_norm = jnp.sqrt(total[own : own + 1] + epsilon)
        query_norm = jnp.sqrt(total[own + 2 : own + 3] + epsilon)
        score = math.sqrt(full_width) * total[own + 1 : own + 2] / (query_norm * row_norm)
        row = lax.broadcasted_iota(jnp.int32, (STAT_ROWS, row_norm.shape[1]), 0)
        columns[q] = jnp.transpose(jnp.where(row == 0, row_norm, score))
        start = pl.multiple_of(pos[1] * own, own)
        mine = columns[q, pl.ds(start, own), :]
        gram = total[0:own] / (mine[:, 0:1] * row_norm)
        gram_out[q] = gram
        penalty_out[q] = gram / (1.0 + jnp.exp(mine[:, 1:2] - score))
        scores[pl.ds(first_query + step * count + q, 1), :] = score


def padded_rows(slab_blocks, block_ids, capacity):
    db_count = lax.axis_size("db")
    blocks_each = slab_blocks.shape[0]
    flat_ids = block_ids.reshape(-1)
    owners = flat_ids // blocks_each
    local_block = flat_ids % blocks_each
    onehot = (owners[:, None] == jnp.arange(db_count, dtype=jnp.int32)[None, :]).astype(jnp.int32)
    slot_index = jnp.sum((jnp.cumsum(onehot, axis=0) - 1) * onehot, axis=1)
    requests = jnp.zeros((db_count, capacity), jnp.int32).at[owners, slot_index].set(local_block)
    found = slab_blocks[lax.all_to_all(requests, "db", split_axis=0, concat_axis=0, tiled=True)]
    replies = lax.all_to_all(found, "db", split_axis=0, concat_axis=0, tiled=True)
    flat_replies = replies.reshape((db_count * capacity,) + slab_blocks.shape[1:])
    return flat_replies[owners * capacity + slot_index]


def per_device(slab, queries, block_ids):
    query_count, width_part = queries.shape
    db_count = lax.axis_size("db")
    pb_count = lax.axis_size("pb")
    blocks_named = block_ids.shape[1]
    cand_count = blocks_named * BLOCK
    own_count = cand_count // pb_count
    blocks_each = slab.shape[0] // BLOCK
    request_count = query_count * blocks_named
    capacity = 3 * request_count // (2 * db_count)
    base = 3 * capacity // 4
    pool_size = 9 * request_count // 128
    partners = db_count - 1
    steps = db_count.bit_length() - 1
    dims = (db_count, capacity, blocks_each, blocks_named, query_count)
    f32, i32 = jnp.float32, jnp.int32
    pos = jnp.stack([lax.axis_index("db"), lax.axis_index("pb")]).astype(i32)
    slab_blocks = slab.reshape(blocks_each, BLOCK, width_part)

    bounds = [0] + [part * base // 36 for part in (17, 26, 32, 36)]
    groups = [
        (1, 0, query_count // 4),
        (2, query_count // 4, query_count // 2),
        (3, query_count // 2, 3 * query_count // 4),
        (4, 3 * query_count // 4, query_count),
    ]
    limit = []
    for needed, first, last in groups:
        limit += [bounds[needed]] * ((last - first) * blocks_named)
    limit = jnp.asarray(limit, i32).reshape(1, request_count)

    ids = block_ids.reshape(1, request_count)
    for step in range(steps):
        ids = jnp.concatenate([ids, exchange(ids, "db", 1 << step)], axis=0)

    def blocks_shape(*sizes):
        return jax.ShapeDtypeStruct(sizes + (BLOCK, width_part), f32)

    size = bounds[1]
    outs = pl.pallas_call(
        functools.partial(index_kernel, dims=dims, base=base, size=size),
        in_specs=[SMEM, VMEM, VMEM, ANY],
        out_specs=[VMEM] * (5 + partners),
        out_shape=[
            jax.ShapeDtypeStruct((capacity, db_count), i32),
            jax.ShapeDtypeStruct((capacity, db_count), i32),
            jax.ShapeDtypeStruct((query_count + 8, db_count), i32),
            jax.ShapeDtypeStruct((pool_size, db_count + 1), i32),
            jax.ShapeDtypeStruct((1, 1), i32),
        ]
        + [blocks_shape(size)] * partners,
        scratch_shapes=[
            pltpu.SMEM((capacity, db_count), i32),
            pltpu.SemaphoreType.DMA,
            pltpu.SemaphoreType.DMA((db_count,)),
        ],
        compiler_params=PARAMS,
        name="index",
    )(pos, ids, limit, slab_blocks)
    table, place, cum, pool, late = outs[:5]
    order = sorted(range(1, db_count), reverse=True)

    def send(chunk):
        got = {}
        for k in order:
            got[k] = exchange(chunk[k - 1], "db", k)
        return [got[k] for k in range(1, db_count)]

    def gather(c, after):
        first, size = bounds[c], bounds[c + 1] - bounds[c]
        tied, _ = lax.optimization_barrier((table, after))
        return pl.pallas_call(
            functools.partial(gather_kernel, first=first, size=size),
            in_specs=[SMEM, ANY],
            out_specs=[VMEM] * partners,
            out_shape=[blocks_shape(size)] * partners,
            scratch_shapes=[pltpu.SemaphoreType.DMA((db_count,))],
            compiler_params=PARAMS,
            name="gather",
        )(tied, slab_blocks)

    def pool_step(step, pooled, after):
        lists = db_count >> (step + 1)
        tied, _ = lax.optimization_barrier((pool, after))
        out = pl.pallas_call(
            functools.partial(pool_kernel, dims=dims, step=step),
            in_specs=[SMEM] + [ANY] * (1 + step),
            out_specs=VMEM,
            out_shape=blocks_shape(lists, pool_size),
            scratch_shapes=[pltpu.SemaphoreType.DMA((lists,))],
            compiler_params=PARAMS,
            name="pool",
        )(tied, slab_blocks, *pooled)
        return out, exchange(out, "db", 1 << step)

    def in_vmem(values):
        return [pltpu.with_memory_space_constraint(value, pltpu.VMEM) for value in values]

    received = [send(outs[5:])]
    pooled = []
    out, got = pool_step(0, pooled, late)
    tied, _ = lax.optimization_barrier((table, out))
    own_rows = pl.pallas_call(
        own_kernel,
        in_specs=[SMEM, ANY],
        out_specs=VMEM,
        out_shape=blocks_shape(capacity),
        scratch_shapes=[pltpu.SemaphoreType.DMA],
        compiler_params=PARAMS,
        name="own",
    )(tied, slab_blocks)
    pooled.append(got)
    chunk = gather(1, out)
    received.append(send(chunk))
    for step in range(1, steps):
        out, got = pool_step(step, pooled, chunk[0])
        pooled.append(got)
    chunk = gather(2, out)
    received.append(send(chunk))
    chunk = gather(3, chunk[0])
    received.append(send(chunk))

    def gram_part(bounds, rows, refs, first, last):
        shape = (last - first, own_count + STAT_ROWS, cand_count)
        halves = ((last - first) * blocks_named, BLOCK, width_part)
        return pl.pallas_call(
            functools.partial(
                gram_kernel,
                dims=dims,
                bounds=bounds,
                first_query=first,
                last_query=last,
            ),
            in_specs=[SMEM] * 4 + [VMEM] * (2 + len(refs)),
            out_specs=[VMEM] * pb_count,
            out_shape=[jax.ShapeDtypeStruct(shape, f32)] * pb_count,
            scratch_shapes=[
                pltpu.VMEM(halves, jnp.bfloat16),
                pltpu.VMEM(halves, jnp.bfloat16),
                pltpu.VMEM((cand_count, cand_count), f32),
            ],
            compiler_params=PARAMS,
            name="gram",
        )(pos, place, cum, pool, queries, *in_vmem([rows, *refs]))

    def finish(parts, first, last, old):
        parts = [parts[0]] + [exchange(parts[j], "pb", j) for j in range(1, pb_count)]
        each = 2 - (last - first) % 2
        part_spec = pl.BlockSpec((each, own_count + STAT_ROWS, cand_count), lambda q: (q, 0, 0))
        out_spec = pl.BlockSpec(
            (each, own_count, cand_count), lambda q: (first // each + q, 0, 0)
        )
        score_spec = pl.BlockSpec((query_count, cand_count), lambda q: (0, 0))
        out_shape = pltpu.HBM((query_count, own_count, cand_count), f32)
        extra = [] if old is None else [score_spec, ANY, ANY]
        aliases = {} if old is None else {pb_count + 2: 1, pb_count + 3: 2}
        return pl.pallas_call(
            functools.partial(
                final_kernel,
                first_query=first,
                full_width=width_part * pb_count,
                parts=pb_count,
                chained=old is not None,
            ),
            grid=((last - first) // each,),
            in_specs=[SMEM] + [part_spec] * pb_count + extra,
            out_specs=[score_spec, out_spec, out_spec],
            out_shape=[jax.ShapeDtypeStruct((query_count, cand_count), f32), out_shape, out_shape],
            scratch_shapes=[pltpu.VMEM((each, cand_count, STAT_ROWS), f32)],
            input_output_aliases=aliases,
            compiler_params=PARAMS,
            name="final",
        )(pos, *parts, *(old or ()))

    results = None
    for needed, first, last in groups:
        refs = [ref for got in received[:needed] for ref in got] + pooled
        parts = gram_part(bounds[: needed + 1], own_rows, refs, first, last)
        results = finish(parts, first, last, results)

    def again(results):
        refs = [ref for got in received for ref in got] + pooled
        parts = gram_part(bounds, own_rows, refs, 0, query_count)
        return finish(parts, 0, query_count, None)

    def padded(results):
        rows = padded_rows(slab_blocks, block_ids, capacity)
        parts = gram_part(None, rows, [], 0, query_count)
        return finish(parts, 0, query_count, None)

    return tuple(lax.switch(late[0, 0], (lambda kept: kept, again, padded), results))


def solution(mesh):
    return jax.shard_map(
        per_device,
        mesh=mesh,
        in_specs=(P("db", "pb"), P("db", "pb"), P("db", None)),
        out_specs=(P("db", None), P("db", "pb", None), P("db", "pb", None)),
        check_vma=False,
    )
```
